256 devices in a mesh: context: 32 (over x, z), mp: 8 (over y, core).
Axes of the slice: x: 4, y: 4, z: 8, core: 2. Of those that a mesh axis runs over, the one named last changes fastest.
Arguments:
- queries: bfloat16 [32768, 2048], P('context', 'mp'), may hold values from -32 to 32
- keys: bfloat16 [32768, 1024], P('context', 'mp'), may hold values from -32 to 32
- values: bfloat16 [32768, 1024], P('context', 'mp'), may hold values from -6 to 6
- out_grad: bfloat16 [32768, 5376], P(('context', 'mp')), may hold values from -24 to 24
- out_weight: bfloat16 [5376, 2048], P(None, 'mp'), may hold values from -0.125 to 0.125
Outputs:
- query_grad: bfloat16 [32768, 2048], P('context', 'mp')
- key_grad: bfloat16 [32768, 1024], P('context', 'mp')
- value_grad: bfloat16 [32768, 1024], P('context', 'mp')
- weight_grad: bfloat16 [5376, 2048], P('context', 'mp')
The draws below stay inside these ranges and needn't reach their ends.
All inputs are finite; a program needn't handle non-finite values.
Results may differ from the reference program's by a relative error of at most 0.02.
Values may be sent and summed in bfloat16 or wider, within the bound.
A program may use at most 128 MiB of HBM per device.

```python
import jax
import jax.numpy as jnp
from jax import lax

D = 5376
QUERY_HEADS = 16
KEY_VALUE_HEADS = 8
HEAD_SIZE = 128
WINDOW_KEYS = 512
SEQUENCE_TOKENS = 32768


def draw_queries(key, part):
    drawn_result = jnp.clip(jax.random.normal(jax.random.fold_in(key, 11), (SEQUENCE_TOKENS, QUERY_HEADS * HEAD_SIZE), jnp.float32), -6.0, 6.0)
    return drawn_result.astype(jnp.bfloat16)


def draw_keys(key, part):
    drawn_result = jnp.clip(jax.random.normal(jax.random.fold_in(key, 12), (SEQUENCE_TOKENS, KEY_VALUE_HEADS * HEAD_SIZE), jnp.float32), -6.0, 6.0)
    return drawn_result.astype(jnp.bfloat16)


def strengthened(drawn, rng, source, target, shards_of, factor):
    def block_of(dim):
        return (jnp.arange(drawn.shape[dim]) // (drawn.shape[dim] // shards_of)).reshape((-1,) + (1,) * (drawn.ndim - 1 - dim))

    first = jax.random.permutation(rng, shards_of)[block_of(target)]
    second = (block_of(target) + shards_of // 2) % shards_of
    return jnp.where((block_of(source) == first) | (block_of(source) == second), factor * drawn, drawn)


def levels(key, dims, shards, smallest, top_value):
    factor_of, own = 1.0, jax.random.fold_in(key, 6)
    for dim, shards_of in shards:
        heights = jnp.exp(jax.random.uniform(jax.random.fold_in(own, dim), (shards_of,), jnp.float32, smallest / len(shards), top_value / len(shards)))
        factor_of = factor_of * jnp.repeat(heights, dims[dim] // shards_of).reshape([-1 if axis == dim else 1 for axis in range(len(dims))])
    return factor_of


def scatter_about(rng, dims, deviation, bound, pieces=(), held_as=jnp.bfloat16):
    drawn = jax.random.normal(rng, dims, jnp.float32) * deviation
    if len(pieces) > 0:
        drawn = levels(rng, dims, pieces, -0.22, 0.18) * drawn
    return jnp.clip(drawn, min=-bound, max=bound).astype(held_as)


def heavy_noise(own_key, shape, spread, bound, split, heavy, held_as=jnp.bfloat16):
    drawn = spread * jax.random.normal(own_key, shape, jnp.float32)
    if split:
        drawn = drawn * levels(own_key, shape, split, -0.22, 0.18)
    return jnp.clip(strengthened(drawn, jax.random.fold_in(own_key, 3), *heavy), -bound, bound).astype(held_as)


def setup_inputs(seed: int = 0) -> dict:
    arg_keys = jax.random.split(jax.random.key(seed), 6)
    queries = draw_queries(jax.random.fold_in(arg_keys[5], 71), 0)
    keys = draw_keys(jax.random.fold_in(arg_keys[5], 71), 0)
    values = scatter_about(arg_keys[2], (SEQUENCE_TOKENS, KEY_VALUE_HEADS * HEAD_SIZE), 1.0, 6.0, ((0, 32), (1, 8)))
    out_grad = heavy_noise(arg_keys[3], (SEQUENCE_TOKENS, D), 1.0, 24.0, ((0, 256),), (0, 1, 256, 6.0))
    out_weight = scatter_about(arg_keys[4], (D, QUERY_HEADS * HEAD_SIZE), (QUERY_HEADS * HEAD_SIZE) ** -0.5, 0.125, ((1, 8),))
    return dict(queries=queries, keys=keys, values=values, out_grad=out_grad, out_weight=out_weight)


SCALE = 168.0 ** -0.5
NEG = -1.0e30


def band_grads(query_rows_block, key_rows_block, value_rows_block, output_grad_rows, key_start):
    rows = query_rows_block.shape[0]
    span = key_rows_block.shape[0]
    qf = query_rows_block.astype(jnp.float32)
    kf = key_rows_block.astype(jnp.float32)
    vf = value_rows_block.astype(jnp.float32)
    df = output_grad_rows.astype(jnp.float32)
    scores = jnp.einsum("qhgd,khd->hgqk", qf, kf, preferred_element_type=jnp.float32) * SCALE
    qpos = jnp.arange(rows, dtype=jnp.int32)[:, None]
    kpos = jnp.arange(span, dtype=jnp.int32)[None, :]
    allowed = (kpos > qpos) & (kpos <= qpos + (span - rows)) & (kpos + key_start >= 0)
    scores = jnp.where(allowed, scores, NEG)
    top = jnp.max(scores, axis=-1, keepdims=True)
    weights = jnp.exp(scores - top)
    prob = weights / jnp.sum(weights, axis=-1, keepdims=True)
    prob_b = prob.astype(jnp.bfloat16)
    pf = prob_b.astype(jnp.float32)
    attn = jnp.einsum("hgqk,khd->qhgd", pf, vf, preferred_element_type=jnp.float32).astype(jnp.bfloat16)
    delta = jnp.sum(df * attn.astype(jnp.float32), axis=-1)
    delta = jnp.transpose(delta, (1, 2, 0))[..., None]
    dprob = jnp.einsum("qhgd,khd->hgqk", df, vf, preferred_element_type=jnp.float32)
    dscore = (prob * (dprob - delta) * SCALE).astype(jnp.bfloat16).astype(jnp.float32)
    dq = jnp.einsum("hgqk,khd->qhgd", dscore, kf, preferred_element_type=jnp.float32)
    key_gradient = jnp.einsum("hgqk,qhgd->khd", dscore, qf, preferred_element_type=jnp.float32)
    value_gradient = jnp.einsum("hgqk,qhgd->khd", pf, df, preferred_element_type=jnp.float32)
    return dq, attn, key_gradient, value_gradient


def reference(queries, keys, values, out_grad, out_weight):
    query_group = QUERY_HEADS // KEY_VALUE_HEADS
    block_index = WINDOW_KEYS // 2
    output_gradient = jnp.dot(out_grad, out_weight, preferred_element_type=jnp.float32).astype(jnp.bfloat16)
    key_padding = jnp.concatenate([jnp.zeros((WINDOW_KEYS, KEY_VALUE_HEADS * HEAD_SIZE), jnp.bfloat16), keys], 0)
    value_padding = jnp.concatenate([jnp.zeros((WINDOW_KEYS, KEY_VALUE_HEADS * HEAD_SIZE), jnp.bfloat16), values], 0)

    def step(carry, index):
        key_gradient_total, value_gradient_total = carry
        start_position = (index * block_index).astype(jnp.int32)
        query_rows_block = lax.dynamic_slice_in_dim(queries, start_position, block_index, 0).reshape(block_index, KEY_VALUE_HEADS, query_group, HEAD_SIZE)
        output_grad_rows = lax.dynamic_slice_in_dim(output_gradient, start_position, block_index, 0).reshape(block_index, KEY_VALUE_HEADS, query_group, HEAD_SIZE)
        key_rows_block = lax.dynamic_slice_in_dim(key_padding, start_position, WINDOW_KEYS + block_index, 0).reshape(WINDOW_KEYS + block_index, KEY_VALUE_HEADS, HEAD_SIZE)
        value_rows_block = lax.dynamic_slice_in_dim(value_padding, start_position, WINDOW_KEYS + block_index, 0).reshape(WINDOW_KEYS + block_index, KEY_VALUE_HEADS, HEAD_SIZE)
        dq, attn, key_gradient, value_gradient = band_grads(query_rows_block, key_rows_block, value_rows_block, output_grad_rows, start_position - WINDOW_KEYS)
        earlier_keys = lax.dynamic_slice_in_dim(key_gradient_total, start_position, WINDOW_KEYS + block_index, 0)
        earlier_values = lax.dynamic_slice_in_dim(value_gradient_total, start_position, WINDOW_KEYS + block_index, 0)
        key_gradient_total = lax.dynamic_update_slice_in_dim(key_gradient_total, earlier_keys + key_gradient.reshape(WINDOW_KEYS + block_index, KEY_VALUE_HEADS * HEAD_SIZE), start_position, 0)
        value_gradient_total = lax.dynamic_update_slice_in_dim(value_gradient_total, earlier_values + value_gradient.reshape(WINDOW_KEYS + block_index, KEY_VALUE_HEADS * HEAD_SIZE), start_position, 0)
        return (key_gradient_total, value_gradient_total), (dq.reshape(block_index, QUERY_HEADS * HEAD_SIZE).astype(jnp.bfloat16), attn.reshape(block_index, QUERY_HEADS * HEAD_SIZE))

    zero_filled = jnp.zeros((WINDOW_KEYS + SEQUENCE_TOKENS, KEY_VALUE_HEADS * HEAD_SIZE), jnp.float32)
    (key_gradient_total, value_gradient_total), (dq_blocks, attn_blocks) = lax.scan(step, (zero_filled, zero_filled), jnp.arange(SEQUENCE_TOKENS // block_index, dtype=jnp.int32))
    query_grad = dq_blocks.reshape(SEQUENCE_TOKENS, QUERY_HEADS * HEAD_SIZE)
    attn_all = attn_blocks.reshape(SEQUENCE_TOKENS, QUERY_HEADS * HEAD_SIZE)
    key_grad = key_gradient_total[WINDOW_KEYS:].astype(jnp.bfloat16)
    value_grad = value_gradient_total[WINDOW_KEYS:].astype(jnp.bfloat16)
    weight_grad = lax.dot_general(out_grad, attn_all, (((0,), (0,)), ((), ())), preferred_element_type=jnp.float32).astype(jnp.bfloat16)
    return query_grad, key_grad, value_grad, weight_grad
```

```python
import jax
import jax.numpy as jnp
from jax import lax
from jax.experimental import pallas as pl
from jax.experimental.pallas import tpu as pltpu
from jax.sharding import PartitionSpec as P

MESH = pl.DeviceIdType.MESH
F32 = jnp.float32
BF16 = jnp.bfloat16

SCALE = 168.0 ** (-0.5)
LOG2E = 1.4426950408889634
NEG = -1e30

SHARD = 1024
HALO = 512
ROWS = 128
SPAN = HALO + ROWS
D = 5376
XS, ZS, YS = 4, 8, 4
BLOCK = D // XS
PIECE = BLOCK // ZS
WIDE = 1408
UNIT = (1408, 1280, 1408, 1280)


def nt(a, b):
    return lax.dot_general(a, b, (((1,), (1,)), ((), ())), preferred_element_type=F32)


def nn(a, b):
    return jnp.dot(a, b, preferred_element_type=F32)


def flipped(a):
    return jnp.transpose(a.astype(F32), (1, 0)).astype(a.dtype)


def kernel(
    q_hbm, k_hbm, v_hbm, g_hbm, w_hbm, dq_hbm, dk_hbm, dv_hbm, dw_hbm,
    q, kf, vf, kt, vt, g, w, prob, at, do, dka, dva, wt, own,
    xs, ha, hb, r1, r2, zs, zr, bs, br, dqv, dkv, dvv, dwv,
    lsem, osem, ag_s, ag_r, halo_s, halo_r, x_s, x_r, z_s, z_r, back_s, back_r,
):
    c = lax.axis_index("context")
    m = lax.axis_index("mp")
    x, z = c // ZS, c % ZS
    y, core = m // 2, m % 2
    up = ((y + 1) % YS) * 2 + core
    down = ((y + YS - 1) % YS) * 2 + core
    far = ((y + 2) % YS) * 2 + core
    sib = y * 2 + (1 - core)
    x1 = x + 1 - 2 * (x % 2)
    x2 = (x + 2) % XS
    x3 = XS - 1 - x
    right = (c + 1) % (XS * ZS)
    left = (c + XS * ZS - 1) % (XS * ZS)

    local = [
        pltpu.make_async_copy(k_hbm, kf.at[pl.ds(HALO, SHARD)], lsem.at[0]),
        pltpu.make_async_copy(v_hbm, vf.at[pl.ds(HALO, SHARD)], lsem.at[1]),
        pltpu.make_async_copy(q_hbm, q, lsem.at[2]),
        pltpu.make_async_copy(g_hbm, g.at[pl.ds(pl.multiple_of(m * ROWS, ROWS), ROWS)], lsem.at[3]),
        pltpu.make_async_copy(w_hbm, w, lsem.at[4]),
    ]
    for copy in local:
        copy.start()

    peers = [(c, up), (c, down), (c, sib), (x1 * ZS + z, m), (x3 * ZS + z, m), (right, m), (left, m)]
    peers += [(x * ZS + (z + d) % ZS, m) for d in range(1, ZS)]
    barrier = pltpu.get_barrier_semaphore()
    for peer in peers:
        pl.semaphore_signal(barrier, inc=1, device_id=peer, device_id_type=MESH)
    pl.semaphore_wait(barrier, len(peers))

    def remote(src, dst, s, r, peer):
        return pltpu.make_async_remote_copy(
            src_ref=src, dst_ref=dst, send_sem=s, recv_sem=r, device_id=peer, device_id_type=MESH
        )

    blocks = (x2, x3, x1, x)

    def wide_start(b):
        return pl.multiple_of((21 * (b // 2) + 10 * (b % 2)) * 128, 128)

    def unit_start(step):
        b = blocks[step]
        if step % 2 == 0:
            return wide_start(b)
        return pl.multiple_of((21 * (b // 2) + 11 * (b % 2)) * 128, 128)

    def rows_of(shard, first, count):
        return pl.ds(pl.multiple_of(shard * ROWS + first, 64), count)

    def ag_copy(step, kind):
        cols = pl.ds(unit_start(step), UNIT[step])
        target = (c, (up, down, up, down, sib, sib, sib, sib, sib)[kind])
        shard, first, count = (
            (m, 0, 128), (m, 0, 128), (down, 0, 64), (up, 64, 64), (m, 0, 128),
            (down, 0, 128), (up, 0, 128), (far, 0, 64), (far, 64, 64),
        )[kind]
        dst = g.at[rows_of(shard, first, count), cols]
        src = g_hbm.at[:, cols] if kind in (0, 1, 4) else dst
        return remote(src, dst, ag_s.at[step, kind], ag_r.at[step, kind], target)

    ag = [[ag_copy(step, kind) for kind in range(9)] for step in range(4)]

    def start(step, *kinds):
        for kind in kinds:
            ag[step][kind].start()

    def arrive(step, *kinds):
        for kind in kinds:
            ag[step][kind].wait_recv()

    def service_near(step):
        arrive(step, 0)
        start(step, 2, 5)
        arrive(step, 1)
        start(step, 3, 6)

    def service_far(step):
        arrive(step, 2)
        start(step, 7)
        arrive(step, 3)
        start(step, 8)

    halo = [
        remote(k_hbm.at[pl.ds(SHARD - HALO, HALO)], kf.at[pl.ds(0, HALO)], halo_s.at[0], halo_r.at[0], (right, m)),
        remote(v_hbm.at[pl.ds(SHARD - HALO, HALO)], vf.at[pl.ds(0, HALO)], halo_s.at[1], halo_r.at[1], (right, m)),
    ]
    start(0, 0, 1)
    for copy in halo:
        copy.start()
    start(0, 4)
    start(1, 0, 1, 4)

    def keys_of(b):
        return pl.ds(pl.multiple_of(b * ROWS, ROWS), SPAN)

    def rows_at(b):
        return pl.ds(pl.multiple_of(b * ROWS, ROWS), ROWS)

    def query_rows(b):
        block = q[rows_at(b), :]
        return jnp.concatenate([block[:, :128], block[:, 128:]], 0)

    key_at = lax.broadcasted_iota(jnp.int32, (ROWS, 2 * ROWS), 0)
    query_at = lax.broadcasted_iota(jnp.int32, (ROWS, 2 * ROWS), 1) % ROWS

    def forward(b, with_halo):
        s = nt(kf[keys_of(b), :], query_rows(b)) * (SCALE * LOG2E)
        s = jnp.concatenate(
            [
                jnp.where(key_at > query_at, s[:ROWS], NEG),
                s[ROWS:HALO],
                jnp.where(key_at <= query_at, s[HALO:], NEG),
            ],
            0,
        )
        if with_halo:
            missing = jnp.where(c == 0, HALO - b * ROWS, 0)
            place = lax.broadcasted_iota(jnp.int32, (SPAN, 2 * ROWS), 0)
            s = jnp.where(place >= missing, s, NEG)
        e = jnp.exp2(s - jnp.max(s, axis=0, keepdims=True))
        p = e * (1.0 / jnp.sum(e, axis=0, keepdims=True))
        prob[b] = p
        a = nn(vt[:, keys_of(b)], p.astype(BF16)).astype(BF16)
        at[:128, rows_at(b)] = a[:, :128]
        at[128:, rows_at(b)] = a[:, 128:]

    for i in (0, 1, 2):
        local[i].wait()
    kt[:, HALO:] = flipped(kf[HALO:, :])
    vt[:, HALO:] = flipped(vf[HALO:, :])

    @pl.loop(4, 8)
    def _(b):
        forward(b, False)

    service_near(0)
    start(2, 0, 1, 4)

    for copy in halo:
        copy.wait_recv()
    kt[:, :HALO] = flipped(kf[:HALO, :])
    vt[:, :HALO] = flipped(vf[:HALO, :])

    @pl.loop(0, 4)
    def _(b):
        forward(b, True)

    service_far(0)
    for i in (3, 4):
        local[i].wait()

    def weight_block(step):
        first = wide_start(blocks[step])
        for o in range(0, WIDE, 256):
            n = min(256, WIDE - o)
            part = nn(at[...], g[:, pl.ds(pl.multiple_of(first + o, 128), n)])
            wt[o : o + n, :] = jnp.transpose(part, (1, 0))

    def piece(step, i):
        b = blocks[step]
        return wt[pl.ds(pl.multiple_of((b % 2) * 64 + i * PIECE, 8), PIECE), :]

    def dout_part(step):
        cols = pl.ds(unit_start(step), UNIT[step])

        @pl.loop(0, 4)
        def _(t):
            rows = pl.ds(pl.multiple_of(t * 256, 256), 256)
            part = nn(g[rows, cols], w[cols, :])
            if step == 0:
                do[rows, :] = part
            else:
                do[rows, :] += part

    x_copies = [
        remote(xs.at[0, pl.ds(0, 4)], ha, x_s.at[0], x_r.at[0], (x1 * ZS + z, m)),
        remote(xs.at[0, pl.ds(4, 4)], hb, x_s.at[1], x_r.at[1], (x3 * ZS + z, m)),
        remote(xs.at[1], r1, x_s.at[2], x_r.at[2], (x3 * ZS + z, m)),
        remote(xs.at[2], r2, x_s.at[3], x_r.at[3], (x1 * ZS + z, m)),
    ]

    service_near(1)
    start(3, 0, 1, 4)
    arrive(0, 4, 5, 6, 7, 8)
    weight_block(0)
    for i in range(ZS):
        xs[0, i] = piece(0, i).astype(BF16)
    x_copies[0].start()
    x_copies[1].start()
    dout_part(0)

    service_far(1)
    service_near(2)
    arrive(1, 4, 5, 6, 7, 8)
    weight_block(1)
    x_copies[0].wait_recv()
    for i in range(ZS):
        t = piece(1, i)
        if i < 4:
            t = t + ha[i].astype(F32)
        xs[1, i] = t.astype(BF16)
    x_copies[2].start()
    dout_part(1)

    service_far(2)
    service_near(3)
    arrive(2, 4, 5, 6, 7, 8)
    weight_block(2)
    x_copies[1].wait_recv()
    for i in range(ZS):
        t = piece(2, i)
        if i >= 4:
            t = t + hb[i - 4].astype(F32)
        xs[2, i] = t.astype(BF16)
    x_copies[3].start()
    dout_part(2)

    service_far(3)
    arrive(3, 4, 5, 6, 7, 8)
    weight_block(3)
    x_copies[2].wait_recv()
    x_copies[3].wait_recv()
    z_copies = []
    for d in (4, 3, 5, 2, 6, 1, 7):
        to = (z + d) % ZS
        zs[to] = (piece(3, to) + r1[to].astype(F32) + r2[to].astype(F32)).astype(BF16)
        copy = remote(zs.at[to], zr.at[d - 1], z_s.at[d - 1], z_r.at[d - 1], (x * ZS + to, m))
        copy.start()
        z_copies.append(copy)
    own[...] = piece(3, z) + r1[z].astype(F32) + r2[z].astype(F32)
    dout_part(3)

    def backward(b):
        qb = query_rows(b)
        block = do[rows_at(b), :].astype(BF16)
        db = jnp.concatenate([block[:, :128], block[:, 128:]], 0)
        dt = jnp.transpose(db.astype(F32), (1, 0))
        a = jnp.concatenate([at[:128, rows_at(b)], at[128:, rows_at(b)]], 1).astype(F32)
        delta = jnp.sum(dt * a, axis=0, keepdims=True)
        p = prob[b]
        ds = (p * (nt(vf[keys_of(b), :], db) - delta)).astype(BF16)
        dqt = nn(kt[:, keys_of(b)], ds) * SCALE
        dqv[rows_at(b), :128] = jnp.transpose(dqt[:, :128], (1, 0)).astype(BF16)
        dqv[rows_at(b), 128:] = jnp.transpose(dqt[:, 128:], (1, 0)).astype(BF16)
        dka[keys_of(b), :] += nn(ds, qb)
        dva[keys_of(b), :] += nn(p.astype(BF16), db)

    dka[...] = jnp.zeros_like(dka)
    dva[...] = jnp.zeros_like(dva)

    @pl.loop(0, 4)
    def _(b):
        backward(b)

    bs[0] = (dka[:HALO, :] * SCALE).astype(BF16)
    bs[1] = dva[:HALO, :].astype(BF16)
    back = remote(bs, br, back_s, back_r, (left, m))
    back.start()

    @pl.loop(4, 8)
    def _(b):
        backward(b)

    outs = [pltpu.make_async_copy(dqv, dq_hbm, osem.at[0])]
    outs[0].start()
    total = own[...]
    for copy, d in zip(z_copies, (4, 3, 5, 2, 6, 1, 7)):
        copy.wait_recv()
        total = total + zr[d - 1].astype(F32)
    dwv[...] = total.astype(BF16)
    outs.append(pltpu.make_async_copy(dwv, dw_hbm, osem.at[1]))
    outs[1].start()
    dkv[:HALO, :] = (dka[HALO:SHARD, :] * SCALE).astype(BF16)
    dvv[:HALO, :] = dva[HALO:SHARD, :].astype(BF16)
    back.wait_recv()
    dkv[HALO:, :] = (dka[SHARD:, :] * SCALE + br[0].astype(F32)).astype(BF16)
    dvv[HALO:, :] = (dva[SHARD:, :] + br[1].astype(F32)).astype(BF16)
    outs.append(pltpu.make_async_copy(dkv, dk_hbm, osem.at[2]))
    outs.append(pltpu.make_async_copy(dvv, dv_hbm, osem.at[3]))
    outs[2].start()
    outs[3].start()
    for step in range(4):
        for kind in range(9):
            ag[step][kind].wait_send()
    for copy in halo + x_copies + z_copies + [back]:
        copy.wait_send()
    for copy in outs:
        copy.wait()


def shards(queries, keys, values, out_grad, out_weight):
    vmem = pltpu.VMEM
    dma = pltpu.SemaphoreType.DMA
    scratch = [
        vmem((SHARD, 256), BF16),
        vmem((HALO + SHARD, 128), BF16),
        vmem((HALO + SHARD, 128), BF16),
        vmem((128, HALO + SHARD), BF16),
        vmem((128, HALO + SHARD), BF16),
        vmem((SHARD, D), BF16),
        vmem((D, 256), BF16),
        vmem((8, SPAN, 256), F32),
        vmem((256, SHARD), BF16),
        vmem((SHARD, 256), F32),
        vmem((HALO + SHARD, 128), F32),
        vmem((HALO + SHARD, 128), F32),
        vmem((WIDE, 256), F32),
        vmem((PIECE, 256), F32),
        vmem((3, ZS, PIECE, 256), BF16),
        vmem((4, PIECE, 256), BF16),
        vmem((4, PIECE, 256), BF16),
        vmem((ZS, PIECE, 256), BF16),
        vmem((ZS, PIECE, 256), BF16),
        vmem((ZS, PIECE, 256), BF16),
        vmem((ZS - 1, PIECE, 256), BF16),
        vmem((2, HALO, 128), BF16),
        vmem((2, HALO, 128), BF16),
        vmem((SHARD, 256), BF16),
        vmem((SHARD, 128), BF16),
        vmem((SHARD, 128), BF16),
        vmem((PIECE, 256), BF16),
        dma((5,)), dma((4,)), dma((4, 9)), dma((4, 9)), dma((2,)), dma((2,)),
        dma((4,)), dma((4,)), dma((7,)), dma((7,)), dma, dma,
    ]
    hbm = pl.BlockSpec(memory_space=pl.ANY)
    return pl.pallas_call(
        kernel,
        out_shape=(
            jax.ShapeDtypeStruct((SHARD, 256), BF16),
            jax.ShapeDtypeStruct((SHARD, 128), BF16),
            jax.ShapeDtypeStruct((SHARD, 128), BF16),
            jax.ShapeDtypeStruct((PIECE, 256), BF16),
        ),
        in_specs=[hbm] * 5,
        out_specs=(hbm,) * 4,
        scratch_shapes=scratch,
        compiler_params=pltpu.CompilerParams(
            collective_id=0, has_side_effects=True, vmem_limit_bytes=56 * 1024 * 1024
        ),
        name="attention_grads",
    )(queries, keys, values, out_grad, out_weight)


def solution(mesh):
    return jax.shard_map(
        shards,
        mesh=mesh,
        in_specs=(
            P("context", "mp"),
            P("context", "mp"),
            P("context", "mp"),
            P(("context", "mp"), None),
            P(None, "mp"),
        ),
        out_specs=(P("context", "mp"), P("context", "mp"), P("context", "mp"), P("context", "mp")),
        check_vma=False,
    )
```

```python
import jax
import jax.numpy as jnp
from jax import lax
from jax.experimental import pallas as pl
from jax.experimental.pallas import tpu as pltpu
from jax.sharding import PartitionSpec as P

MESH = pl.DeviceIdType.MESH
F32 = jnp.float32
BF16 = jnp.bfloat16

SCALE = 168.0 ** (-0.5)
LOG2E = 1.4426950408889634
NEG = -1e30

SHARD = 1024
HALO = 512
ROWS = 128
SPAN = HALO + ROWS
D = 5376
XS, ZS, YS = 4, 8, 4
PIECE = D // (XS * ZS)
BLOCK = XS * PIECE
WIDE = 768
STEPS = ZS
ENDS = tuple(-(-BLOCK * (s + 1) // 128) * 128 for s in range(STEPS))
BEGINS = (0,) + ENDS[:-1]
AHEAD = 2


def nt(a, b):
    return lax.dot_general(a, b, (((1,), (1,)), ((), ())), preferred_element_type=F32)


def nn(a, b):
    return jnp.dot(a, b, preferred_element_type=F32)


def flipped(a):
    return jnp.transpose(a.astype(F32), (1, 0)).astype(a.dtype)


def kernel(
    q_hbm, k_hbm, v_hbm, g_hbm, w_hbm, dq_hbm, dk_hbm, dv_hbm, dw_hbm,
    q, kf, vf, kt, vt, gown, g, wp, wf, wb, prob, at, do, dka, dva, wt,
    as_, bs_, ar, br, sx, fs, fr, hs, hr, dqv, dkv, dvv, dwv,
    lsem, osem, ag_s, ag_r, halo_s, halo_r, za_s, za_r, zb_s, zb_r, x_s, x_r, back_s, back_r,
):
    c = lax.axis_index("context")
    m = lax.axis_index("mp")
    x, z = c // ZS, c % ZS
    y, core = m // 2, m % 2
    up = ((y + 1) % YS) * 2 + core
    down = ((y + YS - 1) % YS) * 2 + core
    far = ((y + 2) % YS) * 2 + core
    sib = y * 2 + (1 - core)
    right = (c + 1) % (XS * ZS)
    left = (c + XS * ZS - 1) % (XS * ZS)
    above = x * ZS + (z + 1) % ZS
    below = x * ZS + (z + ZS - 1) % ZS

    def target_z(z, step, i):
        return (z + ZS - 1 - step) % ZS if i < 2 else (z + 1 + step) % ZS

    local = [
        pltpu.make_async_copy(g_hbm, gown, lsem.at[0]),
        pltpu.make_async_copy(k_hbm, kf.at[pl.ds(HALO, SHARD)], lsem.at[1]),
        pltpu.make_async_copy(v_hbm, vf.at[pl.ds(HALO, SHARD)], lsem.at[2]),
        pltpu.make_async_copy(q_hbm, q, lsem.at[3]),
        pltpu.make_async_copy(w_hbm, wp, lsem.at[4]),
    ]
    for copy in local:
        copy.start()
    peers = [(c, up), (c, down), (c, sib), (above, m), (below, m), (right, m), (left, m)]
    peers += [(((x + e) % XS) * ZS + z, m) for e in range(1, XS)]
    barrier = pltpu.get_barrier_semaphore()
    for peer in peers:
        pl.semaphore_signal(barrier, inc=1, device_id=peer, device_id_type=MESH)
    def reorder(first, last):
        for zz in range(ZS):

            @pl.when(z == zz)
            def _():
                @pl.loop(0, ROWS // 16)
                def _(t):
                    rows = pl.ds(pl.multiple_of(t * 16, 16), 16)
                    out_rows = pl.ds(pl.multiple_of(m * ROWS + t * 16, 16), 16)
                    for tile in range(first // 128, last // 128):
                        parts = []
                        at_col = tile * 128
                        while at_col < tile * 128 + 128:
                            n, inside = at_col // PIECE, at_col % PIECE
                            count = min(PIECE - inside, tile * 128 + 128 - at_col)
                            step, i = n // XS, n % XS
                            begin = (i * ZS + target_z(zz, step, i)) * PIECE + inside
                            while count > 0:
                                part = min(count, 128 - begin % 128)
                                base = begin // 128 * 128
                                tile_in = gown[rows, base : base + 128].astype(F32)
                                parts.append(tile_in[:, begin % 128 : begin % 128 + part])
                                begin += part
                                at_col += part
                                count -= part
                        g[out_rows, tile * 128 : tile * 128 + 128] = (
                            parts[0] if len(parts) == 1 else jnp.concatenate(parts, 1)
                        ).astype(BF16)

    def remote(src, dst, s, r, peer):
        return pltpu.make_async_remote_copy(
            src_ref=src, dst_ref=dst, send_sem=s, recv_sem=r, device_id=peer, device_id_type=MESH
        )

    def ag_copy(step, kind):
        target = (c, (up, down, up, down, sib, sib, sib, sib, sib)[kind])
        shard, first, count = (
            (m, 0, 128), (m, 0, 128), (down, 0, 64), (up, 64, 64), (m, 0, 128),
            (down, 0, 128), (up, 0, 128), (far, 0, 64), (far, 64, 64),
        )[kind]
        rows = pl.ds(pl.multiple_of(shard * ROWS + first, 64), count)
        part = g.at[rows, pl.ds(BEGINS[step], ENDS[step] - BEGINS[step])]
        return remote(part, part, ag_s.at[step, kind], ag_r.at[step, kind], target)

    ag = [[ag_copy(step, kind) for kind in range(9)] for step in range(STEPS)]

    def start(step, *kinds):
        for kind in kinds:
            ag[step][kind].start()

    def arrive(step, *kinds):
        for kind in kinds:
            ag[step][kind].wait_recv()

    def service_near(step):
        arrive(step, 0)
        start(step, 2, 5)
        arrive(step, 1)
        start(step, 3, 6)
        if step + AHEAD < STEPS:
            start(step + AHEAD, 0, 1, 4)

    def service_far(step):
        arrive(step, 2)
        start(step, 7)
        arrive(step, 3)
        start(step, 8)

    halo = [
        remote(k_hbm.at[pl.ds(SHARD - HALO, HALO)], kf.at[pl.ds(0, HALO)], halo_s.at[0], halo_r.at[0], (right, m)),
        remote(v_hbm.at[pl.ds(SHARD - HALO, HALO)], vf.at[pl.ds(0, HALO)], halo_s.at[1], halo_r.at[1], (right, m)),
    ]
    local[0].wait()
    reorder(BEGINS[0], ENDS[0])
    pl.semaphore_wait(barrier, len(peers))
    start(0, 0, 1)
    for copy in halo:
        copy.start()
    start(0, 4)
    reorder(BEGINS[1], ENDS[1])
    start(1, 0, 1, 4)
    reorder(BEGINS[2], ENDS[STEPS - 1])

    def keys_of(b):
        return pl.ds(pl.multiple_of(b * ROWS, ROWS), SPAN)

    def rows_at(b):
        return pl.ds(pl.multiple_of(b * ROWS, ROWS), ROWS)

    def query_rows(b):
        block = q[rows_at(b), :]
        return jnp.concatenate([block[:, :128], block[:, 128:]], 0)

    key_at = lax.broadcasted_iota(jnp.int32, (ROWS, 2 * ROWS), 0)
    query_at = lax.broadcasted_iota(jnp.int32, (ROWS, 2 * ROWS), 1) % ROWS

    def forward(b, with_halo):
        s = nt(kf[keys_of(b), :], query_rows(b)) * (SCALE * LOG2E)
        s = jnp.concatenate(
            [
                jnp.where(key_at > query_at, s[:ROWS], NEG),
                s[ROWS:HALO],
                jnp.where(key_at <= query_at, s[HALO:], NEG),
            ],
            0,
        )
        if with_halo:
            missing = jnp.where(c == 0, HALO - b * ROWS, 0)
            place = lax.broadcasted_iota(jnp.int32, (SPAN, 2 * ROWS), 0)
            s = jnp.where(place >= missing, s, NEG)
        e = jnp.exp2(s - jnp.max(s, axis=0, keepdims=True))
        p = e * (1.0 / jnp.sum(e, axis=0, keepdims=True))
        prob[b] = p
        a = nn(vt[:, keys_of(b)], p.astype(BF16)).astype(BF16)
        at[:128, rows_at(b)] = a[:, :128]
        at[128:, rows_at(b)] = a[:, 128:]

    for i in (1, 2, 3):
        local[i].wait()
    kt[:, HALO:] = flipped(kf[HALO:, :])
    vt[:, HALO:] = flipped(vf[HALO:, :])

    @pl.loop(4, 8)
    def _(b):
        forward(b, False)

    service_near(0)
    for copy in halo:
        copy.wait_recv()
    kt[:, :HALO] = flipped(kf[:HALO, :])
    vt[:, :HALO] = flipped(vf[:HALO, :])

    @pl.loop(0, 4)
    def _(b):
        forward(b, True)

    service_far(0)
    service_near(1)
    local[4].wait()
    wf[...] = wp[...].astype(F32)

    @pl.loop(0, STEPS)
    def _(step):
        for half in (0, 2):
            two = []
            for i in (half, half + 1):
                p = i * ZS + target_z(z, step, i)
                two.append(wf[pl.ds(pl.multiple_of(p * PIECE, 8), PIECE), :])
            rows = pl.ds(pl.multiple_of(step * BLOCK + half * PIECE, 16), 2 * PIECE)
            wb[rows, :] = jnp.concatenate(two, 0).astype(BF16)

    def dout_part(step):
        cols = slice(BEGINS[step], ENDS[step])

        @pl.loop(0, 4)
        def _(t):
            rows = pl.ds(pl.multiple_of(t * 256, 256), 256)
            part = nn(g[rows, cols], wb[cols, :])
            if step == 0:
                do[rows, :] = part
            else:
                do[rows, :] += part

    z_copies = []

    def weight_part(step):
        first = step * BLOCK // 128 * 128
        for o in range(0, WIDE, 256):
            part = nn(at[...], g[:, first + o : first + o + 256])
            wt[o : o + 256, :] = jnp.transpose(part, (1, 0))
        if step > 0:
            for copy in z_copies[-2:]:
                copy.wait_recv()
        for i in range(XS):
            begin = step * BLOCK - first + i * PIECE
            t = wt[begin : begin + PIECE, :]
            if step > 0:
                t = t + (ar[step - 1, i] if i < 2 else br[step - 1, i - 2]).astype(F32)
            if step == STEPS - 1:
                sx[i] = t
                fs[i] = t.astype(BF16)
            elif i < 2:
                as_[step, i] = t.astype(BF16)
            else:
                bs_[step, i - 2] = t.astype(BF16)
        if step < STEPS - 1:
            z_copies.append(remote(as_.at[step], ar.at[step], za_s.at[step], za_r.at[step], (above, m)))
            z_copies.append(remote(bs_.at[step], br.at[step], zb_s.at[step], zb_r.at[step], (below, m)))
            for copy in z_copies[-2:]:
                copy.start()

    for step in range(STEPS):
        if step > 0:
            service_far(step)
        if 0 < step < STEPS - 1:
            service_near(step + 1)
        arrive(step, 4, 5, 6, 7, 8)
        weight_part(step)
        if step < STEPS - 1:
            dout_part(step)

    x_copies = []
    for e in (2, 1, 3):
        to = (x + e) % XS
        x_copies.append(remote(fs.at[to], fr.at[e - 1], x_s.at[e - 1], x_r.at[e - 1], (to * ZS + z, m)))
        x_copies[-1].start()
    dout_part(STEPS - 1)

    def backward(b):
        qb = query_rows(b)
        block = do[rows_at(b), :].astype(BF16)
        db = jnp.concatenate([block[:, :128], block[:, 128:]], 0)
        dt = jnp.transpose(db.astype(F32), (1, 0))
        a = jnp.concatenate([at[:128, rows_at(b)], at[128:, rows_at(b)]], 1).astype(F32)
        delta = jnp.sum(dt * a, axis=0, keepdims=True)
        p = prob[b]
        ds = (p * (nt(vf[keys_of(b), :], db) - delta)).astype(BF16)
        dqt = nn(kt[:, keys_of(b)], ds) * SCALE
        dqv[rows_at(b), :128] = jnp.transpose(dqt[:, :128], (1, 0)).astype(BF16)
        dqv[rows_at(b), 128:] = jnp.transpose(dqt[:, 128:], (1, 0)).astype(BF16)
        dka[keys_of(b), :] += nn(ds, qb)
        dva[keys_of(b), :] += nn(p.astype(BF16), db)

    dka[...] = jnp.zeros_like(dka)
    dva[...] = jnp.zeros_like(dva)

    def back(b):
        return remote(hs.at[b], hr.at[b], back_s.at[b], back_r.at[b], (left, m))

    @pl.loop(0, 4)
    def _(b):
        backward(b)
        hs[b, 0] = (dka[rows_at(b), :] * SCALE).astype(BF16)
        hs[b, 1] = dva[rows_at(b), :].astype(BF16)
        back(b).start()

    @pl.loop(4, 8)
    def _(b):
        backward(b)

    outs = [pltpu.make_async_copy(dqv, dq_hbm, osem.at[0])]
    outs[0].start()
    total = sx[x]
    for copy, e in zip(x_copies, (2, 1, 3)):
        copy.wait_recv()
        total = total + fr[e - 1].astype(F32)
    dwv[...] = total.astype(BF16)
    outs.append(pltpu.make_async_copy(dwv, dw_hbm, osem.at[1]))
    outs[1].start()
    dkv[:HALO, :] = (dka[HALO:SHARD, :] * SCALE).astype(BF16)
    dvv[:HALO, :] = dva[HALO:SHARD, :].astype(BF16)
    for b in range(4):
        back(b).wait_recv()
        rows = slice(HALO + b * ROWS, HALO + (b + 1) * ROWS)
        late = slice(SHARD + b * ROWS, SHARD + (b + 1) * ROWS)
        dkv[rows, :] = (dka[late, :] * SCALE + hr[b, 0].astype(F32)).astype(BF16)
        dvv[rows, :] = (dva[late, :] + hr[b, 1].astype(F32)).astype(BF16)
    outs.append(pltpu.make_async_copy(dkv, dk_hbm, osem.at[2]))
    outs.append(pltpu.make_async_copy(dvv, dv_hbm, osem.at[3]))
    outs[2].start()
    outs[3].start()
    for step in range(STEPS):
        for kind in range(9):
            ag[step][kind].wait_send()
    for copy in halo + z_copies + x_copies + [back(b) for b in range(4)]:
        copy.wait_send()
    for copy in outs:
        copy.wait()


def hand_on(*refs):
    ins, outs, held, sem = refs[:4], refs[4:8], refs[8:12], refs[12]
    first = [pltpu.make_async_copy(ins[i], held[i], sem.at[0, i]) for i in range(4)]
    second = [pltpu.make_async_copy(held[i], outs[i], sem.at[1, i]) for i in range(4)]
    for copy in first:
        copy.start()
    for i in (3, 1, 2, 0):
        first[i].wait()
        second[i].start()
    for copy in second:
        copy.wait()


def shards(queries, keys, values, out_grad, out_weight):
    vmem = pltpu.VMEM
    dma = pltpu.SemaphoreType.DMA
    scratch = [
        vmem((SHARD, 256), BF16),
        vmem((HALO + SHARD, 128), BF16),
        vmem((HALO + SHARD, 128), BF16),
        vmem((128, HALO + SHARD), BF16),
        vmem((128, HALO + SHARD), BF16),
        vmem((ROWS, D), BF16),
        vmem((SHARD, D), BF16),
        vmem((D, 256), BF16),
        vmem((D, 256), F32),
        vmem((D, 256), BF16),
        vmem((8, SPAN, 256), F32),
        vmem((256, SHARD), BF16),
        vmem((SHARD, 256), F32),
        vmem((HALO + SHARD, 128), F32),
        vmem((HALO + SHARD, 128), F32),
        vmem((WIDE, 256), F32),
        vmem((STEPS - 1, 2, PIECE, 256), BF16),
        vmem((STEPS - 1, 2, PIECE, 256), BF16),
        vmem((STEPS - 1, 2, PIECE, 256), BF16),
        vmem((STEPS - 1, 2, PIECE, 256), BF16),
        vmem((XS, PIECE, 256), F32),
        vmem((XS, PIECE, 256), BF16),
        vmem((XS - 1, PIECE, 256), BF16),
        vmem((4, 2, ROWS, 128), BF16),
        vmem((4, 2, ROWS, 128), BF16),
        vmem((SHARD, 256), BF16),
        vmem((SHARD, 128), BF16),
        vmem((SHARD, 128), BF16),
        vmem((PIECE, 256), BF16),
        dma((5,)), dma((4,)), dma((STEPS, 9)), dma((STEPS, 9)), dma((2,)), dma((2,)),
        dma((7,)), dma((7,)), dma((7,)), dma((7,)), dma((3,)), dma((3,)), dma((4,)), dma((4,)),
    ]
    hbm = pl.BlockSpec(memory_space=pl.ANY)
    shapes = (
        jax.ShapeDtypeStruct((SHARD, 256), BF16),
        jax.ShapeDtypeStruct((SHARD, 128), BF16),
        jax.ShapeDtypeStruct((SHARD, 128), BF16),
        jax.ShapeDtypeStruct((PIECE, 256), BF16),
    )
    grads = pl.pallas_call(
        kernel,
        out_shape=shapes,
        in_specs=[hbm] * 5,
        out_specs=(hbm,) * 4,
        scratch_shapes=scratch,
        compiler_params=pltpu.CompilerParams(
            collective_id=0, has_side_effects=True, vmem_limit_bytes=58 * 1024 * 1024
        ),
        name="attention_grads",
    )(queries, keys, values, out_grad, out_weight)
    return pl.pallas_call(
        hand_on,
        out_shape=shapes,
        in_specs=[hbm] * 4,
        out_specs=(hbm,) * 4,
        scratch_shapes=[vmem(s.shape, BF16) for s in shapes] + [dma((2, 4))],
        name="hand_on",
    )(*grads)


def solution(mesh):
    return jax.shard_map(
        shards,
        mesh=mesh,
        in_specs=(
            P("context", "mp"),
            P("context", "mp"),
            P("context", "mp"),
            P(("context", "mp"), None),
            P(None, "mp"),
        ),
        out_specs=(P("context", "mp"), P("context", "mp"), P("context", "mp"), P("context", "mp")),
        check_vma=False,
    )
```

```python
import jax
import jax.numpy as jnp
from jax import lax
from jax.experimental import pallas as pl
from jax.experimental.pallas import tpu as pltpu
from jax.sharding import PartitionSpec as P

MESH = pl.DeviceIdType.MESH
F32 = jnp.float32
BF16 = jnp.bfloat16

SCALE = 168.0 ** (-0.5)
LOG2E = 1.4426950408889634
NEG = -1e30

SHARD = 1024
HALO = 512
ROWS = 128
SPAN = HALO + ROWS
D = 5376
XS, ZS, YS = 4, 8, 4
PIECE = D // (XS * ZS)
BLOCK = XS * PIECE
WIDE = 768
STEPS = ZS
ENDS = tuple(-(-BLOCK * (s + 1) // 128) * 128 for s in range(STEPS))
BEGINS = (0,) + ENDS[:-1]
AHEAD = 2
AWAY = (4, -3, 3, -2, 2, -1, 1, 0)
ADDS = ((), (), (0,), (1,), (2,), (3,), (4,), (5, 6))
PAIR = 2 * ROWS


def nt(a, b):
    return lax.dot_general(a, b, (((1,), (1,)), ((), ())), preferred_element_type=F32)


def nn(a, b):
    return jnp.dot(a, b, preferred_element_type=F32)


def flipped(a):
    return jnp.transpose(a.astype(F32), (1, 0)).astype(a.dtype)


def kernel(
    q_hbm, k_hbm, v_hbm, g_hbm, w_hbm, dqv, dkv, dvv, dwv,
    q, kf, vf, kt, vt, gown, g, wp, wf, wb, prob, at, do, dn, dka, dva, wt,
    as_, bs_, ar, br, sx, fs, fr, hs, hr,
    lsem, ag_s, ag_r, halo_s, halo_r, za_s, za_r, zb_s, zb_r, x_s, x_r, back_s, back_r,
):
    c = lax.axis_index("context")
    m = lax.axis_index("mp")
    x, z = c // ZS, c % ZS
    y, core = m // 2, m % 2
    up = ((y + 1) % YS) * 2 + core
    down = ((y + YS - 1) % YS) * 2 + core
    far = ((y + 2) % YS) * 2 + core
    sib = y * 2 + (1 - core)
    right = (c + 1) % (XS * ZS)
    left = (c + XS * ZS - 1) % (XS * ZS)
    above = x * ZS + (z + 1) % ZS
    below = x * ZS + (z + ZS - 1) % ZS

    def target_z(z, step, i):
        away = AWAY[step] if i < 2 else -AWAY[step]
        return (z + away + ZS) % ZS

    local = [
        pltpu.make_async_copy(g_hbm, gown, lsem.at[0]),
        pltpu.make_async_copy(k_hbm, kf.at[pl.ds(HALO, SHARD)], lsem.at[1]),
        pltpu.make_async_copy(v_hbm, vf.at[pl.ds(HALO, SHARD)], lsem.at[2]),
        pltpu.make_async_copy(q_hbm, q, lsem.at[3]),
        pltpu.make_async_copy(w_hbm, wp, lsem.at[4]),
    ]
    for copy in local:
        copy.start()
    peers = [(c, up), (c, down), (c, sib), (above, m), (below, m), (right, m), (left, m)]
    peers += [(((x + e) % XS) * ZS + z, m) for e in range(1, XS)]
    barrier = pltpu.get_barrier_semaphore()
    for peer in peers:
        pl.semaphore_signal(barrier, inc=1, device_id=peer, device_id_type=MESH)
    def reorder(first, last):
        for zz in range(ZS):

            @pl.when(z == zz)
            def _():
                @pl.loop(0, ROWS // 16)
                def _(t):
                    rows = pl.ds(pl.multiple_of(t * 16, 16), 16)
                    out_rows = pl.ds(pl.multiple_of(m * ROWS + t * 16, 16), 16)
                    for tile in range(first // 128, last // 128):
                        parts = []
                        at_col = tile * 128
                        while at_col < tile * 128 + 128:
                            n, inside = at_col // PIECE, at_col % PIECE
                            count = min(PIECE - inside, tile * 128 + 128 - at_col)
                            step, i = n // XS, n % XS
                            begin = (i * ZS + target_z(zz, step, i)) * PIECE + inside
                            while count > 0:
                                part = min(count, 128 - begin % 128)
                                base = begin // 128 * 128
                                tile_in = gown[rows, base : base + 128].astype(F32)
                                parts.append(tile_in[:, begin % 128 : begin % 128 + part])
                                begin += part
                                at_col += part
                                count -= part
                        g[out_rows, tile * 128 : tile * 128 + 128] = (
                            parts[0] if len(parts) == 1 else jnp.concatenate(parts, 1)
                        ).astype(BF16)

    def remote(src, dst, s, r, peer):
        return pltpu.make_async_remote_copy(
            src_ref=src, dst_ref=dst, send_sem=s, recv_sem=r, device_id=peer, device_id_type=MESH
        )

    def ag_copy(step, kind):
        target = (c, (up, down, up, down, sib, sib, sib, sib, sib)[kind])
        shard, first, count = (
            (m, 0, 128), (m, 0, 128), (down, 0, 64), (up, 64, 64), (m, 0, 128),
            (down, 0, 128), (up, 0, 128), (far, 0, 64), (far, 64, 64),
        )[kind]
        rows = pl.ds(pl.multiple_of(shard * ROWS + first, 64), count)
        part = g.at[rows, pl.ds(BEGINS[step], ENDS[step] - BEGINS[step])]
        return remote(part, part, ag_s.at[step, kind], ag_r.at[step, kind], target)

    ag = [[ag_copy(step, kind) for kind in range(9)] for step in range(STEPS)]

    def start(step, *kinds):
        for kind in kinds:
            ag[step][kind].start()

    def arrive(step, *kinds):
        for kind in kinds:
            ag[step][kind].wait_recv()

    def service_near(step):
        arrive(step, 0)
        start(step, 2, 5)
        arrive(step, 1)
        start(step, 3, 6)
        if step + AHEAD < STEPS:
            start(step + AHEAD, 0, 1)

    def service_far(step):
        arrive(step, 2)
        start(step, 7)
        arrive(step, 3)
        start(step, 8)

    halo = [
        remote(k_hbm.at[pl.ds(SHARD - HALO, HALO)], kf.at[pl.ds(0, HALO)], halo_s.at[0], halo_r.at[0], (right, m)),
        remote(v_hbm.at[pl.ds(SHARD - HALO, HALO)], vf.at[pl.ds(0, HALO)], halo_s.at[1], halo_r.at[1], (right, m)),
    ]
    local[0].wait()
    reorder(BEGINS[0], ENDS[0])
    pl.semaphore_wait(barrier, len(peers))
    start(0, 0, 1)
    for copy in halo:
        copy.start()
    start(0, 4)
    reorder(BEGINS[1], ENDS[1])
    start(1, 0, 1, 4)
    reorder(BEGINS[2], ENDS[STEPS - 1])
    for step in range(2, STEPS):
        start(step, 4)

    def keys_of(b):
        return pl.ds(pl.multiple_of(b * ROWS, ROWS), SPAN)

    def rows_at(b):
        return pl.ds(pl.multiple_of(b * ROWS, ROWS), ROWS)

    def query_rows(b):
        block = q[rows_at(b), :]
        return jnp.concatenate([block[:, :128], block[:, 128:]], 0)

    key_at = lax.broadcasted_iota(jnp.int32, (ROWS, 2 * ROWS), 0)
    query_at = lax.broadcasted_iota(jnp.int32, (ROWS, 2 * ROWS), 1) % ROWS

    def forward(b, with_halo):
        s = nt(kf[keys_of(b), :], query_rows(b)) * (SCALE * LOG2E)
        s = jnp.concatenate(
            [
                jnp.where(key_at > query_at, s[:ROWS], NEG),
                s[ROWS:HALO],
                jnp.where(key_at <= query_at, s[HALO:], NEG),
            ],
            0,
        )
        if with_halo:
            missing = jnp.where(c == 0, HALO - b * ROWS, 0)
            place = lax.broadcasted_iota(jnp.int32, (SPAN, 2 * ROWS), 0)
            s = jnp.where(place >= missing, s, NEG)
        e = jnp.exp2(s - jnp.max(s, axis=0, keepdims=True))
        p = e * (1.0 / jnp.sum(e, axis=0, keepdims=True))
        prob[b] = p
        a = nn(vt[:, keys_of(b)], p.astype(BF16)).astype(BF16)
        at[:128, rows_at(b)] = a[:, :128]
        at[128:, rows_at(b)] = a[:, 128:]

    for i in (1, 2, 3):
        local[i].wait()
    kt[:, HALO:] = flipped(kf[HALO:, :])
    vt[:, HALO:] = flipped(vf[HALO:, :])

    @pl.loop(4, 8)
    def _(b):
        forward(b, False)

    service_near(0)
    for copy in halo:
        copy.wait_recv()
    kt[:, :HALO] = flipped(kf[:HALO, :])
    vt[:, :HALO] = flipped(vf[:HALO, :])

    @pl.loop(0, 4)
    def _(b):
        forward(b, True)

    service_far(0)
    service_near(1)
    local[4].wait()
    wf[...] = wp[...].astype(F32)

    for step in range(STEPS):
        for half in (0, 2):
            two = []
            for i in (half, half + 1):
                p = i * ZS + target_z(z, step, i)
                two.append(wf[pl.ds(pl.multiple_of(p * PIECE, 8), PIECE), :])
            begin = step * BLOCK + half * PIECE
            wb[begin : begin + 2 * PIECE, :] = jnp.concatenate(two, 0).astype(BF16)

    def dout_part(step):
        part = nn(g[:, BEGINS[step] : ENDS[step]], wb[BEGINS[step] : ENDS[step], :])
        if step == 0:
            do[...] = part
        else:
            do[...] += part

    def pair_rows(chip):
        return pl.ds(pl.multiple_of(chip * PAIR, PAIR), PAIR)

    dka[...] = jnp.zeros_like(dka)
    dva[...] = jnp.zeros_like(dva)
    z_copies = []

    def weight_product(step):
        first = step * BLOCK // 128 * 128
        for o in range(0, WIDE, 256):
            part = nn(at[...], g[:, first + o : first + o + 256])
            wt[o : o + 256, :] = jnp.transpose(part, (1, 0))

    def weight_sums(step):
        first = step * BLOCK // 128 * 128
        for before in ADDS[step]:
            for copy in z_copies[2 * before : 2 * before + 2]:
                copy.wait_recv()
        for i in range(XS):
            begin = step * BLOCK - first + i * PIECE
            t = wt[begin : begin + PIECE, :]
            for before in ADDS[step]:
                t = t + (ar[before, i] if i < 2 else br[before, i - 2]).astype(F32)
            if step == STEPS - 1:
                sx[i] = t
                fs[i] = t.astype(BF16)
            elif i < 2:
                as_[step, i] = t.astype(BF16)
            else:
                bs_[step, i - 2] = t.astype(BF16)
        if step < STEPS - 1:
            one, other = (above, below) if AWAY[step] > 0 else (below, above)
            z_copies.append(remote(as_.at[step], ar.at[step], za_s.at[step], za_r.at[step], (one, m)))
            z_copies.append(remote(bs_.at[step], br.at[step], zb_s.at[step], zb_r.at[step], (other, m)))
            for copy in z_copies[-2:]:
                copy.start()

    def backward(b, dout, first):
        qb = query_rows(b)
        block = dout[pl.ds(pl.multiple_of(first, ROWS), ROWS), :].astype(BF16)
        db = jnp.concatenate([block[:, :128], block[:, 128:]], 0)
        dt = jnp.transpose(db.astype(F32), (1, 0))
        a = jnp.concatenate([at[:128, rows_at(b)], at[128:, rows_at(b)]], 1).astype(F32)
        delta = jnp.sum(dt * a, axis=0, keepdims=True)
        p = prob[b]
        ds = (p * (nt(vf[keys_of(b), :], db) - delta)).astype(BF16)
        dqt = nn(kt[:, keys_of(b)], ds) * SCALE
        dqv[rows_at(b), :128] = jnp.transpose(dqt[:, :128], (1, 0)).astype(BF16)
        dqv[rows_at(b), 128:] = jnp.transpose(dqt[:, 128:], (1, 0)).astype(BF16)
        dka[keys_of(b), :] += nn(ds, qb)
        dva[keys_of(b), :] += nn(p.astype(BF16), db)

    def back(b):
        return remote(hs.at[b], hr.at[b], back_s.at[b], back_r.at[b], (left, m))

    def send_back(*pieces):
        for b in pieces:
            hs[b, 0] = (dka[rows_at(b), :] * SCALE).astype(BF16)
            hs[b, 1] = dva[rows_at(b), :].astype(BF16)
            back(b).start()

    for step in range(STEPS - 1):
        if step > 0:
            service_near(step + 1)
            service_far(step)
        arrive(step, 5, 6, 7, 8)
        if step == 0:
            for later in range(STEPS):
                arrive(later, 4)
        weight_product(step)
        weight_sums(step)
        if step == STEPS - 2:
            service_far(step + 1)
        dout_part(step)
        if step == 2:
            dn[...] = nn(g[pair_rows(y), :], wb[...])
        if step == 3:

            @pl.loop(0, 2)
            def _(t):
                backward(y * 2 + t, dn, t * ROWS)

    last = STEPS - 1
    opposite = (y + 2) % YS
    near = (y + 1) % 2

    def chip_tokens(chip):
        cols = slice(BEGINS[last], ENDS[last])
        do[pair_rows(chip), :] += nn(g[pair_rows(chip), cols], wb[cols, :])

        @pl.loop(0, 2)
        def _(t):
            backward(chip * 2 + t, do, chip * PAIR + t * ROWS)

    arrive(last, 5, 6)
    chip_tokens(near)

    @pl.when(y != 2)
    def _():
        send_back(0, 1)

    @pl.when(y < 2)
    def _():
        send_back(2, 3)

    arrive(last, 7, 8)
    do[pair_rows(opposite), :] += nn(
        g[pair_rows(opposite), BEGINS[last] : ENDS[last]], wb[BEGINS[last] : ENDS[last], :]
    )
    backward(opposite * 2, do, opposite * PAIR)

    @pl.when(y == 2)
    def _():
        send_back(0)

    backward(opposite * 2 + 1, do, opposite * PAIR + ROWS)

    @pl.when(y == 2)
    def _():
        send_back(1)

    @pl.when(y >= 2)
    def _():
        send_back(2, 3)

    weight_product(last)
    weight_sums(last)
    x_copies = []
    for e in (2, 1, 3):
        to = (x + e) % XS
        x_copies.append(remote(fs.at[to], fr.at[e - 1], x_s.at[e - 1], x_r.at[e - 1], (to * ZS + z, m)))
        x_copies[-1].start()
    chip_tokens(near + 2)
    total = sx[x]
    for copy, e in zip(x_copies, (2, 1, 3)):
        copy.wait_recv()
        total = total + fr[e - 1].astype(F32)
    dwv[...] = total.astype(BF16)
    dkv[:HALO, :] = (dka[HALO:SHARD, :] * SCALE).astype(BF16)
    dvv[:HALO, :] = dva[HALO:SHARD, :].astype(BF16)
    for b in range(4):
        back(b).wait_recv()
        rows = slice(HALO + b * ROWS, HALO + (b + 1) * ROWS)
        late = slice(SHARD + b * ROWS, SHARD + (b + 1) * ROWS)
        dkv[rows, :] = (dka[late, :] * SCALE + hr[b, 0].astype(F32)).astype(BF16)
        dvv[rows, :] = (dva[late, :] + hr[b, 1].astype(F32)).astype(BF16)
    for step in range(STEPS):
        for kind in range(9):
            ag[step][kind].wait_send()
    for copy in halo + z_copies + x_copies + [back(b) for b in range(4)]:
        copy.wait_send()


def hand_on(*refs):
    copies = [pltpu.make_async_copy(refs[i], refs[4 + i], refs[8].at[i]) for i in range(4)]
    for copy in copies:
        copy.start()
    for copy in copies:
        copy.wait()


def shards(queries, keys, values, out_grad, out_weight):
    vmem = pltpu.VMEM
    dma = pltpu.SemaphoreType.DMA
    scratch = [
        vmem((SHARD, 256), BF16),
        vmem((HALO + SHARD, 128), BF16),
        vmem((HALO + SHARD, 128), BF16),
        vmem((128, HALO + SHARD), BF16),
        vmem((128, HALO + SHARD), BF16),
        vmem((ROWS, D), BF16),
        vmem((SHARD, D), BF16),
        vmem((D, 256), BF16),
        vmem((D, 256), F32),
        vmem((D, 256), BF16),
        vmem((8, SPAN, 256), F32),
        vmem((256, SHARD), BF16),
        vmem((SHARD, 256), F32),
        vmem((PAIR, 256), F32),
        vmem((HALO + SHARD, 128), F32),
        vmem((HALO + SHARD, 128), F32),
        vmem((WIDE, 256), F32),
        vmem((STEPS - 1, 2, PIECE, 256), BF16),
        vmem((STEPS - 1, 2, PIECE, 256), BF16),
        vmem((STEPS - 1, 2, PIECE, 256), BF16),
        vmem((STEPS - 1, 2, PIECE, 256), BF16),
        vmem((XS, PIECE, 256), F32),
        vmem((XS, PIECE, 256), BF16),
        vmem((XS - 1, PIECE, 256), BF16),
        vmem((4, 2, ROWS, 128), BF16),
        vmem((4, 2, ROWS, 128), BF16),
        dma((5,)), dma((STEPS, 9)), dma((STEPS, 9)), dma((2,)), dma((2,)),
        dma((7,)), dma((7,)), dma((7,)), dma((7,)), dma((3,)), dma((3,)), dma((4,)), dma((4,)),
    ]
    hbm = pl.BlockSpec(memory_space=pl.ANY)
    shapes = (
        jax.ShapeDtypeStruct((SHARD, 256), BF16),
        jax.ShapeDtypeStruct((SHARD, 128), BF16),
        jax.ShapeDtypeStruct((SHARD, 128), BF16),
        jax.ShapeDtypeStruct((PIECE, 256), BF16),
    )
    grads = pl.pallas_call(
        kernel,
        out_shape=tuple(vmem(s.shape, s.dtype) for s in shapes),
        in_specs=[hbm] * 5,
        out_specs=(pl.BlockSpec(memory_space=vmem),) * 4,
        scratch_shapes=scratch,
        compiler_params=pltpu.CompilerParams(
            collective_id=0, has_side_effects=True, vmem_limit_bytes=58 * 1024 * 1024
        ),
        name="attention_grads",
    )(queries, keys, values, out_grad, out_weight)
    return pl.pallas_call(
        hand_on,
        out_shape=shapes,
        in_specs=[pl.BlockSpec(memory_space=vmem)] * 4,
        out_specs=(hbm,) * 4,
        scratch_shapes=[dma((4,))],
        name="hand_on",
    )(*[pltpu.with_memory_space_constraint(g, vmem) for g in grads])


def solution(mesh):
    return jax.shard_map(
        shards,
        mesh=mesh,
        in_specs=(
            P("context", "mp"),
            P("context", "mp"),
            P("context", "mp"),
            P(("context", "mp"), None),
            P(None, "mp"),
        ),
        out_specs=(P("context", "mp"), P("context", "mp"), P("context", "mp"), P("context", "mp")),
        check_vma=False,
    )
```

```python
import jax
import jax.numpy as jnp
from jax import lax
from jax.experimental import pallas as pl
from jax.experimental.pallas import tpu as pltpu
from jax.sharding import PartitionSpec as P

MESH = pl.DeviceIdType.MESH
F32 = jnp.float32
BF16 = jnp.bfloat16

SCALE = 168.0 ** (-0.5)
LOG2E = 1.4426950408889634
NEG = -1e30

SHARD = 1024
HALO = 512
ROWS = 128
SPAN = HALO + ROWS
D = 5376
XS, ZS, YS = 4, 8, 4
PIECE = D // (XS * ZS)
BLOCK = XS * PIECE
WIDE = 768
STEPS = ZS
ENDS = tuple(-(-BLOCK * (s + 1) // 128) * 128 for s in range(STEPS))
BEGINS = (0,) + ENDS[:-1]
AHEAD = 2
AWAY = (4, -3, 3, -2, 2, -1, 1, 0)
ADDS = ((), (), (0,), (1,), (2,), (3,), (4,), (5, 6))
PAIR = 2 * ROWS


def nt(a, b):
    return lax.dot_general(a, b, (((1,), (1,)), ((), ())), preferred_element_type=F32)


def nn(a, b):
    return jnp.dot(a, b, preferred_element_type=F32)


def flipped(a):
    return jnp.transpose(a.astype(F32), (1, 0)).astype(a.dtype)


def kernel(
    q_hbm, k_hbm, v_hbm, g_hbm, w_hbm, dqv, dkv, dvv, dwv,
    q, kf, vf, kt, vt, gown, g, wp, wf, wb, prob, at, do, dn, dka, dva, wt,
    as_, bs_, ar, br, sx, fs, fr, hs, hr,
    lsem, ag_s, ag_r, halo_s, halo_r, za_s, za_r, zb_s, zb_r, x_s, x_r, back_s, back_r,
):
    c = lax.axis_index("context")
    m = lax.axis_index("mp")
    x, z = c // ZS, c % ZS
    y, core = m // 2, m % 2
    up = ((y + 1) % YS) * 2 + core
    down = ((y + YS - 1) % YS) * 2 + core
    far = ((y + 2) % YS) * 2 + core
    sib = y * 2 + (1 - core)
    right = (c + 1) % (XS * ZS)
    left = (c + XS * ZS - 1) % (XS * ZS)
    above = x * ZS + (z + 1) % ZS
    below = x * ZS + (z + ZS - 1) % ZS

    def target_z(z, step, i):
        away = AWAY[step] if i < 2 else -AWAY[step]
        return (z + away + ZS) % ZS

    local = [
        pltpu.make_async_copy(g_hbm, gown, lsem.at[0]),
        pltpu.make_async_copy(k_hbm, kf.at[pl.ds(HALO, SHARD)], lsem.at[1]),
        pltpu.make_async_copy(v_hbm, vf.at[pl.ds(HALO, SHARD)], lsem.at[2]),
        pltpu.make_async_copy(q_hbm, q, lsem.at[3]),
        pltpu.make_async_copy(w_hbm, wp, lsem.at[4]),
    ]
    local[0].start()
    peers = [(c, up), (c, down), (c, sib), (above, m), (below, m), (right, m), (left, m)]
    peers += [(((x + e) % XS) * ZS + z, m) for e in range(1, XS)]
    barrier = pltpu.get_barrier_semaphore()
    for peer in peers:
        pl.semaphore_signal(barrier, inc=1, device_id=peer, device_id_type=MESH)
    def reorder(first, last):
        for zz in range(ZS):

            @pl.when(z == zz)
            def _():
                @pl.loop(0, ROWS // 16)
                def _(t):
                    rows = pl.ds(pl.multiple_of(t * 16, 16), 16)
                    out_rows = pl.ds(pl.multiple_of(m * ROWS + t * 16, 16), 16)
                    for tile in range(first // 128, last // 128):
                        parts = []
                        at_col = tile * 128
                        while at_col < tile * 128 + 128:
                            n, inside = at_col // PIECE, at_col % PIECE
                            count = min(PIECE - inside, tile * 128 + 128 - at_col)
                            step, i = n // XS, n % XS
                            begin = (i * ZS + target_z(zz, step, i)) * PIECE + inside
                            while count > 0:
                                part = min(count, 128 - begin % 128)
                                base = begin // 128 * 128
                                tile_in = gown[rows, base : base + 128].astype(F32)
                                parts.append(tile_in[:, begin % 128 : begin % 128 + part])
                                begin += part
                                at_col += part
                                count -= part
                        g[out_rows, tile * 128 : tile * 128 + 128] = (
                            parts[0] if len(parts) == 1 else jnp.concatenate(parts, 1)
                        ).astype(BF16)

    def remote(src, dst, s, r, peer):
        return pltpu.make_async_remote_copy(
            src_ref=src, dst_ref=dst, send_sem=s, recv_sem=r, device_id=peer, device_id_type=MESH
        )

    def ag_copy(step, kind):
        target = (c, (up, down, up, down, sib, sib, sib, sib, sib)[kind])
        shard, first, count = (
            (m, 0, 128), (m, 0, 128), (down, 0, 64), (up, 64, 64), (m, 0, 128),
            (down, 0, 128), (up, 0, 128), (far, 0, 64), (far, 64, 64),
        )[kind]
        rows = pl.ds(pl.multiple_of(shard * ROWS + first, 64), count)
        part = g.at[rows, pl.ds(BEGINS[step], ENDS[step] - BEGINS[step])]
        return remote(part, part, ag_s.at[step, kind], ag_r.at[step, kind], target)

    ag = [[ag_copy(step, kind) for kind in range(9)] for step in range(STEPS)]

    def start(step, *kinds):
        for kind in kinds:
            ag[step][kind].start()

    def arrive(step, *kinds):
        for kind in kinds:
            ag[step][kind].wait_recv()

    def sent(*steps):
        for step in steps:
            for kind in range(9):
                ag[step][kind].wait_send()

    def service_near(step):
        arrive(step, 0)
        start(step, 2)
        if step + AHEAD < STEPS:
            start(step + AHEAD, 0)
        start(step, 5)
        arrive(step, 1)
        start(step, 3)
        if step + AHEAD < STEPS:
            start(step + AHEAD, 1)
        start(step, 6)

    def service_far(step):
        arrive(step, 2)
        start(step, 7)
        arrive(step, 3)
        start(step, 8)

    halo = [
        remote(k_hbm.at[pl.ds(SHARD - HALO, HALO)], kf.at[pl.ds(0, HALO)], halo_s.at[0], halo_r.at[0], (right, m)),
        remote(v_hbm.at[pl.ds(SHARD - HALO, HALO)], vf.at[pl.ds(0, HALO)], halo_s.at[1], halo_r.at[1], (right, m)),
    ]
    local[0].wait()
    for copy in local[1:]:
        copy.start()
    reorder(BEGINS[0], ENDS[0])
    pl.semaphore_wait(barrier, len(peers))
    start(0, 0, 1)
    for copy in halo:
        copy.start()
    start(0, 4)
    reorder(BEGINS[1], ENDS[1])
    start(1, 0, 1, 4)
    reorder(BEGINS[2], ENDS[STEPS - 1])
    for step in range(2, STEPS):
        start(step, 4)

    def keys_of(b):
        return pl.ds(pl.multiple_of(b * ROWS, ROWS), SPAN)

    def rows_at(b):
        return pl.ds(pl.multiple_of(b * ROWS, ROWS), ROWS)

    def query_rows(b):
        block = q[rows_at(b), :]
        return jnp.concatenate([block[:, :128], block[:, 128:]], 0)

    key_at = lax.broadcasted_iota(jnp.int32, (ROWS, 2 * ROWS), 0)
    query_at = lax.broadcasted_iota(jnp.int32, (ROWS, 2 * ROWS), 1) % ROWS

    def forward(b, with_halo):
        s = nt(kf[keys_of(b), :], query_rows(b)) * (SCALE * LOG2E)
        s = jnp.concatenate(
            [
                jnp.where(key_at > query_at, s[:ROWS], NEG),
                s[ROWS:HALO],
                jnp.where(key_at <= query_at, s[HALO:], NEG),
            ],
            0,
        )
        if with_halo:
            missing = jnp.where(c == 0, HALO - b * ROWS, 0)
            place = lax.broadcasted_iota(jnp.int32, (SPAN, 2 * ROWS), 0)
            s = jnp.where(place >= missing, s, NEG)
        e = jnp.exp2(s - jnp.max(s, axis=0, keepdims=True))
        p = e * (1.0 / jnp.sum(e, axis=0, keepdims=True))
        prob[b] = p
        a = nn(vt[:, keys_of(b)], p.astype(BF16)).astype(BF16)
        at[:128, rows_at(b)] = a[:, :128]
        at[128:, rows_at(b)] = a[:, 128:]

    for i in (1, 2, 3):
        local[i].wait()
    kt[:, HALO:] = flipped(kf[HALO:, :])
    vt[:, HALO:] = flipped(vf[HALO:, :])

    @pl.loop(4, 8)
    def _(b):
        forward(b, False)

    service_near(0)
    for copy in halo:
        copy.wait_recv()
    kt[:, :HALO] = flipped(kf[:HALO, :])
    vt[:, :HALO] = flipped(vf[:HALO, :])

    @pl.loop(0, 4)
    def _(b):
        forward(b, True)

    service_far(0)
    service_near(1)
    local[4].wait()
    wf[...] = wp[...].astype(F32)

    for step in range(STEPS):
        for half in (0, 2):
            two = []
            for i in (half, half + 1):
                p = i * ZS + target_z(z, step, i)
                two.append(wf[pl.ds(pl.multiple_of(p * PIECE, 8), PIECE), :])
            begin = step * BLOCK + half * PIECE
            wb[begin : begin + 2 * PIECE, :] = jnp.concatenate(two, 0).astype(BF16)

    def dout_part(step):
        part = nn(g[:, BEGINS[step] : ENDS[step]], wb[BEGINS[step] : ENDS[step], :])
        if step == 0:
            do[...] = part
        else:
            do[...] += part

    def pair_rows(chip):
        return pl.ds(pl.multiple_of(chip * PAIR, PAIR), PAIR)

    dka[...] = jnp.zeros_like(dka)
    dva[...] = jnp.zeros_like(dva)
    z_copies = []

    def weight_product(step):
        first = step * BLOCK // 128 * 128
        for o in range(0, WIDE, 256):
            part = nn(at[...], g[:, first + o : first + o + 256])
            wt[o : o + 256, :] = jnp.transpose(part, (1, 0))

    def weight_sums(step):
        first = step * BLOCK // 128 * 128
        for before in ADDS[step]:
            for copy in z_copies[2 * before : 2 * before + 2]:
                copy.wait_recv()
        for i in range(XS):
            begin = step * BLOCK - first + i * PIECE
            t = wt[begin : begin + PIECE, :]
            for before in ADDS[step]:
                t = t + (ar[before, i] if i < 2 else br[before, i - 2]).astype(F32)
            if step == STEPS - 1:
                sx[i] = t
                fs[i] = t.astype(BF16)
            elif i < 2:
                as_[step, i] = t.astype(BF16)
            else:
                bs_[step, i - 2] = t.astype(BF16)
        if step < STEPS - 1:
            one, other = (above, below) if AWAY[step] > 0 else (below, above)
            z_copies.append(remote(as_.at[step], ar.at[step], za_s.at[step], za_r.at[step], (one, m)))
            z_copies.append(remote(bs_.at[step], br.at[step], zb_s.at[step], zb_r.at[step], (other, m)))
            for copy in z_copies[-2:]:
                copy.start()

    def backward(b, dout, first):
        qb = query_rows(b)
        block = dout[pl.ds(pl.multiple_of(first, ROWS), ROWS), :].astype(BF16)
        db = jnp.concatenate([block[:, :128], block[:, 128:]], 0)
        dt = jnp.transpose(db.astype(F32), (1, 0))
        a = jnp.concatenate([at[:128, rows_at(b)], at[128:, rows_at(b)]], 1).astype(F32)
        delta = jnp.sum(dt * a, axis=0, keepdims=True)
        p = prob[b]
        ds = (p * (nt(vf[keys_of(b), :], db) - delta)).astype(BF16)
        dqt = nn(kt[:, keys_of(b)], ds) * SCALE
        dqv[rows_at(b), :128] = jnp.transpose(dqt[:, :128], (1, 0)).astype(BF16)
        dqv[rows_at(b), 128:] = jnp.transpose(dqt[:, 128:], (1, 0)).astype(BF16)
        dka[keys_of(b), :] += nn(ds, qb)
        dva[keys_of(b), :] += nn(p.astype(BF16), db)

    def back(b):
        return remote(hs.at[b], hr.at[b], back_s.at[b], back_r.at[b], (left, m))

    def send_back(*pieces):
        for b in pieces:
            hs[b, 0] = (dka[rows_at(b), :] * SCALE).astype(BF16)
            hs[b, 1] = dva[rows_at(b), :].astype(BF16)
            back(b).start()

    for step in range(STEPS - 1):
        if step > 0:
            service_near(step + 1)
            service_far(step)
        arrive(step, 5, 6, 7, 8)
        if step == 0:
            for later in range(STEPS):
                arrive(later, 4)
        weight_product(step)
        weight_sums(step)
        if step == STEPS - 2:
            service_far(step + 1)
        dout_part(step)
        if step > 1:
            sent(step - 2)
        if step == 2:
            dn[...] = nn(g[pair_rows(y), :], wb[...])
        if step == 3:

            @pl.loop(0, 2)
            def _(t):
                backward(y * 2 + t, dn, t * ROWS)

    last = STEPS - 1
    opposite = (y + 2) % YS
    near = (y + 1) % 2

    def chip_tokens(chip):
        cols = slice(BEGINS[last], ENDS[last])
        do[pair_rows(chip), :] += nn(g[pair_rows(chip), cols], wb[cols, :])

        @pl.loop(0, 2)
        def _(t):
            backward(chip * 2 + t, do, chip * PAIR + t * ROWS)

    arrive(last, 5, 6)
    chip_tokens(near)

    @pl.when(y != 2)
    def _():
        send_back(0, 1)

    @pl.when(y < 2)
    def _():
        send_back(2, 3)

    arrive(last, 7, 8)
    do[pair_rows(opposite), :] += nn(
        g[pair_rows(opposite), BEGINS[last] : ENDS[last]], wb[BEGINS[last] : ENDS[last], :]
    )
    backward(opposite * 2, do, opposite * PAIR)

    @pl.when(y == 2)
    def _():
        send_back(0)

    backward(opposite * 2 + 1, do, opposite * PAIR + ROWS)

    @pl.when(y == 2)
    def _():
        send_back(1)

    @pl.when(y >= 2)
    def _():
        send_back(2, 3)

    weight_product(last)
    sent(STEPS - 3, STEPS - 2)
    weight_sums(last)
    x_copies = []
    for e in (2, 1, 3):
        to = (x + e) % XS
        x_copies.append(remote(fs.at[to], fr.at[e - 1], x_s.at[e - 1], x_r.at[e - 1], (to * ZS + z, m)))
        x_copies[-1].start()
    sent(last)
    for copy in halo + z_copies:
        copy.wait_send()
    chip_tokens(near + 2)
    total = sx[x]
    for copy, e in zip(x_copies, (2, 1, 3)):
        copy.wait_recv()
        total = total + fr[e - 1].astype(F32)
    dwv[...] = total.astype(BF16)
    dkv[:HALO, :] = (dka[HALO:SHARD, :] * SCALE).astype(BF16)
    dvv[:HALO, :] = dva[HALO:SHARD, :].astype(BF16)
    for b in range(4):
        back(b).wait_recv()
        rows = slice(HALO + b * ROWS, HALO + (b + 1) * ROWS)
        late = slice(SHARD + b * ROWS, SHARD + (b + 1) * ROWS)
        dkv[rows, :] = (dka[late, :] * SCALE + hr[b, 0].astype(F32)).astype(BF16)
        dvv[rows, :] = (dva[late, :] + hr[b, 1].astype(F32)).astype(BF16)
    for copy in x_copies + [back(b) for b in range(4)]:
        copy.wait_send()


def hand_on(*refs):
    copies = [pltpu.make_async_copy(refs[i], refs[4 + i], refs[8].at[i]) for i in range(4)]
    for copy in copies:
        copy.start()
    for copy in copies:
        copy.wait()


def shards(queries, keys, values, out_grad, out_weight):
    vmem = pltpu.VMEM
    dma = pltpu.SemaphoreType.DMA
    scratch = [
        vmem((SHARD, 256), BF16),
        vmem((HALO + SHARD, 128), BF16),
        vmem((HALO + SHARD, 128), BF16),
        vmem((128, HALO + SHARD), BF16),
        vmem((128, HALO + SHARD), BF16),
        vmem((ROWS, D), BF16),
        vmem((SHARD, D), BF16),
        vmem((D, 256), BF16),
        vmem((D, 256), F32),
        vmem((D, 256), BF16),
        vmem((8, SPAN, 256), F32),
        vmem((256, SHARD), BF16),
        vmem((SHARD, 256), F32),
        vmem((PAIR, 256), F32),
        vmem((HALO + SHARD, 128), F32),
        vmem((HALO + SHARD, 128), F32),
        vmem((WIDE, 256), F32),
        vmem((STEPS - 1, 2, PIECE, 256), BF16),
        vmem((STEPS - 1, 2, PIECE, 256), BF16),
        vmem((STEPS - 1, 2, PIECE, 256), BF16),
        vmem((STEPS - 1, 2, PIECE, 256), BF16),
        vmem((XS, PIECE, 256), F32),
        vmem((XS, PIECE, 256), BF16),
        vmem((XS - 1, PIECE, 256), BF16),
        vmem((4, 2, ROWS, 128), BF16),
        vmem((4, 2, ROWS, 128), BF16),
        dma((5,)), dma((STEPS, 9)), dma((STEPS, 9)), dma((2,)), dma((2,)),
        dma((7,)), dma((7,)), dma((7,)), dma((7,)), dma((3,)), dma((3,)), dma((4,)), dma((4,)),
    ]
    hbm = pl.BlockSpec(memory_space=pl.ANY)
    shapes = (
        jax.ShapeDtypeStruct((SHARD, 256), BF16),
        jax.ShapeDtypeStruct((SHARD, 128), BF16),
        jax.ShapeDtypeStruct((SHARD, 128), BF16),
        jax.ShapeDtypeStruct((PIECE, 256), BF16),
    )
    grads = pl.pallas_call(
        kernel,
        out_shape=tuple(vmem(s.shape, s.dtype) for s in shapes),
        in_specs=[hbm] * 5,
        out_specs=(pl.BlockSpec(memory_space=vmem),) * 4,
        scratch_shapes=scratch,
        compiler_params=pltpu.CompilerParams(
            collective_id=0, has_side_effects=True, vmem_limit_bytes=58 * 1024 * 1024
        ),
        name="attention_grads",
    )(queries, keys, values, out_grad, out_weight)
    return pl.pallas_call(
        hand_on,
        out_shape=shapes,
        in_specs=[pl.BlockSpec(memory_space=vmem)] * 4,
        out_specs=(hbm,) * 4,
        scratch_shapes=[dma((4,))],
        name="hand_on",
    )(*[pltpu.with_memory_space_constraint(g, vmem) for g in grads])


def solution(mesh):
    return jax.shard_map(
        shards,
        mesh=mesh,
        in_specs=(
            P("context", "mp"),
            P("context", "mp"),
            P("context", "mp"),
            P(("context", "mp"), None),
            P(None, "mp"),
        ),
        out_specs=(P("context", "mp"), P("context", "mp"), P("context", "mp"), P("context", "mp")),
        check_vma=False,
    )
```
